512 devices in a mesh: dp: 4 (over x), seq: 16 (over z, core), tensor: 8 (over y).
Axes of the slice: x: 4, y: 8, z: 8, core: 2. Of those that a mesh axis runs over, the one named last changes fastest.
Arguments:
- hidden: bfloat16 [8192, 8192], P(('dp', 'seq'), 'tensor'), may hold values from -6 to 6
- queries: bfloat16 [8192, 8192], P(('dp', 'seq'), 'tensor'), may hold values from -14 to 14
- kv_weight: bfloat16 [8192, 2048], P('seq', 'tensor'), may hold values from -0.0625 to 0.0625
- parents: int32 [4, 16], P('dp'), may hold values from -1 to 14, as said below
- out_grad: bfloat16 [8192, 8192], P(('dp', 'seq'), 'tensor'), may hold values from -6 to 6
Outputs:
- attended: bfloat16 [8192, 8192], P(('dp', 'seq'), 'tensor')
- query_grad: float32 [8192, 8192], P(('dp', 'seq'), 'tensor')
- weight_grad: float32 [8192, 2048], P('seq', 'tensor')
The draws below stay inside these ranges and needn't reach their ends.
Inputs may be any that keep to these rules, and one draw needn't show every extreme that they name: parents[g, n] is -1 where node block n begins a new tree of group g (always for n = 0), else an earlier node block of the same group; the last node block of every group has parent 16 - 2.
All inputs are finite; a program needn't handle non-finite values.
Results may differ from the reference program's by a relative error of at most 0.012.
The reference program's roundings to bfloat16 on the way count: a program that leaves them out, or rounds other values in their place, can miss the bound.
Values may be sent and summed in bfloat16 or wider, within the bound.
No kernel may reach another device: no remote copies, remote signals or barrier semaphores. Data moves between devices by JAX's collectives and lax.ppermute only.
A program may use at most 64 MiB of HBM per device.

```python
import math
import jax
import jax.numpy as jnp
from jax import lax

D = 8192
HEADS = 64
KVH = 8
HD = 128
TOK_DEV = 128
NODES = 16
GROUPS = 4
TOKENS = 8192


def draw_queries(key, part):
    shape_pair = (TOKENS, HEADS * HD)
    drawn = jax.random.truncated_normal(key, -6.0, 6.0, shape_pair, jnp.float32)
    return drawn.astype(jnp.bfloat16)


def draw_parents(key, part):
    key_flag, key_pick = jax.random.split(key)
    root_flags = jax.random.randint(key_flag, (GROUPS, NODES), 0, 4)
    parent_picks = jax.random.randint(key_pick, (GROUPS, NODES), 0, 1 << 20)
    node_ids = jnp.arange(NODES, dtype=jnp.int32)[None, :]
    chosen = parent_picks % jnp.maximum(node_ids, 1)
    drawn = jnp.where((node_ids == 0) | (root_flags == 0), -1, chosen)
    drawn = jnp.where(node_ids == NODES - 1, NODES - 2, drawn)
    return drawn.astype(jnp.int32)


def block_levels(own_key, dims, pieces, smallest, largest):
    loudness = 1.0
    for position, parts in pieces:
        heights = jax.random.uniform(jax.random.fold_in(jax.random.fold_in(own_key, 6), position), (parts,), jnp.float32, smallest / len(pieces), largest / len(pieces))
        loudness = loudness * jnp.repeat(jnp.exp(heights), dims[position] // parts).reshape((-1,) + (1,) * (len(dims) - 1 - position))
    return loudness


def scatter_about(own_key, dims, scale, reach, cuts=(), kind=jnp.bfloat16):
    values = scale * jax.random.normal(own_key, dims, jnp.float32)
    if cuts:
        values = values * block_levels(own_key, dims, cuts, -0.22, 0.18)
    return jnp.clip(values, -reach, reach).astype(kind)


def setup_inputs(seed: int = 0) -> dict:
    arg_keys = jax.random.split(jax.random.key(seed), 6)
    return {
        "hidden": scatter_about(arg_keys[0], (TOKENS, D), 1.0, 6.0, ((0, 64), (1, 8))),
        "queries": draw_queries(jax.random.fold_in(arg_keys[5], 71), 0),
        "kv_weight": scatter_about(arg_keys[2], (D, KVH * 2 * HD), D ** -0.5, 0.0625, ((0, 16), (1, 8))),
        "parents": draw_parents(jax.random.fold_in(arg_keys[5], 71), 0),
        "out_grad": scatter_about(arg_keys[4], (TOKENS, HEADS * HD), 1.0, 6.0, ((0, 64), (1, 8))),
    }


def ancestor_table(parent_row):
    node_ids = jnp.arange(NODES, dtype=jnp.int32)

    def follow(state_pair, unused_item):
        current, marked = state_pair
        marked = jnp.maximum(marked, (current[:, None] == node_ids[None, :]).astype(jnp.int32))
        current = jnp.where(current >= 0, parent_row[jnp.maximum(current, 0)], -1).astype(jnp.int32)
        return ((current, marked), None)
    start_state = (parent_row.astype(jnp.int32), jnp.zeros((NODES, NODES), jnp.int32))
    final_state, unused_out = lax.scan(follow, start_state, None, length=NODES)
    return final_state[1]

def block_terms(query_blk, grad_blk, keys_all, values_all, visible):
    inv_root = 1.0 / math.sqrt(HD)
    scores = jnp.einsum('tkgd,jkd->kgtj', query_blk, keys_all) * inv_root
    scores = jnp.where(visible[None, None], scores, -jnp.inf)
    row_top = lax.optimization_barrier(jnp.max(scores, axis=-1, keepdims=True))
    expons = jnp.exp(scores - row_top)
    probs_f = expons / lax.optimization_barrier(jnp.sum(expons, axis=-1, keepdims=True))
    weights = lax.optimization_barrier(probs_f.astype(jnp.bfloat16)).astype(jnp.float32)
    mixed_f = jnp.einsum('kgtj,jkd->tkgd', weights, values_all)
    prob_grad = jnp.einsum('tkgd,jkd->kgtj', grad_blk, values_all)
    inner_sum = jnp.transpose(lax.optimization_barrier(jnp.sum(grad_blk * mixed_f, axis=-1)), (1, 2, 0))
    score_grad = probs_f * (prob_grad - inner_sum[..., None]) * inv_root
    score_grad = lax.optimization_barrier(score_grad.astype(jnp.bfloat16)).astype(jnp.float32)
    query_grad = jnp.einsum('kgtj,jkd->tkgd', score_grad, keys_all)
    key_grad = jnp.einsum('kgtj,tkgd->jkd', score_grad, query_blk)
    value_grad = jnp.einsum('kgtj,tkgd->jkd', weights, grad_blk)
    return (mixed_f, query_grad, jnp.stack([key_grad, value_grad], axis=2))

def reference(hidden, queries, kv_weight, parents, out_grad):
    group_tok = NODES * TOK_DEV
    heads_per = HEADS // KVH
    hidden_groups = hidden.reshape(GROUPS, group_tok, D)
    query_groups = queries.reshape(GROUPS, group_tok, HEADS * HD)
    grad_groups = out_grad.reshape(GROUPS, group_tok, HEADS * HD)
    key_node = jnp.arange(group_tok, dtype=jnp.int32) // TOK_DEV
    key_pos = jnp.arange(group_tok, dtype=jnp.int32) % TOK_DEV
    query_pos = jnp.arange(TOK_DEV, dtype=jnp.int32)

    def per_group(weight_sum, group_args):
        x_group, q_group, g_group, parent_row = group_args
        kv_group = jnp.dot(x_group, kv_weight, preferred_element_type=jnp.float32).astype(jnp.bfloat16)
        kv_split = kv_group.astype(jnp.float32).reshape(group_tok, KVH, 2, HD)
        keys_all = kv_split[:, :, 0, :]
        values_all = kv_split[:, :, 1, :]
        marked = ancestor_table(parent_row)

        def per_node(grad_sum, node_index):
            first_row = node_index * TOK_DEV
            query_blk = lax.dynamic_slice_in_dim(q_group, first_row, TOK_DEV, 0).astype(jnp.float32)
            query_blk = query_blk.reshape(TOK_DEV, KVH, heads_per, HD)
            grad_blk = lax.dynamic_slice_in_dim(g_group, first_row, TOK_DEV, 0).astype(jnp.float32)
            grad_blk = grad_blk.reshape(TOK_DEV, KVH, heads_per, HD)
            above_keys = marked[node_index][key_node] > 0
            visible = above_keys[None, :] | (key_node == node_index)[None, :] & (key_pos[None, :] <= query_pos[:, None])
            mixed_f, query_grad, kv_terms = block_terms(query_blk, grad_blk, keys_all, values_all, visible)
            rounded = lax.optimization_barrier(kv_terms.astype(jnp.bfloat16)).astype(jnp.float32)
            outputs = (mixed_f.astype(jnp.bfloat16).reshape(TOK_DEV, HEADS * HD), query_grad.reshape(TOK_DEV, HEADS * HD))
            return (grad_sum + rounded, outputs)
        grad_sum, (mixed_all, query_all) = lax.scan(per_node, jnp.zeros((group_tok, KVH, 2, HD), jnp.float32), jnp.arange(NODES, dtype=jnp.int32))
        kv_grad = grad_sum.astype(jnp.bfloat16).reshape(group_tok, KVH * 2 * HD)
        weight_term = jnp.dot(x_group.T, kv_grad, preferred_element_type=jnp.float32)
        return (weight_sum + weight_term, (mixed_all.reshape(group_tok, HEADS * HD), query_all.reshape(group_tok, HEADS * HD)))
    weight_sum, (attended, query_grad) = lax.scan(per_group, jnp.zeros((D, KVH * 2 * HD), jnp.float32), (hidden_groups, query_groups, grad_groups, parents))
    return (attended.reshape(TOKENS, HEADS * HD), query_grad.reshape(TOKENS, HEADS * HD), weight_sum / (GROUPS * NODES))
```

```python
import math

import jax
import jax.numpy as jnp
from jax import lax
from jax.experimental import pallas as pl
from jax.experimental.pallas import tpu as pltpu
from jax.sharding import Mesh, PartitionSpec as P

HD = 128
TOK = 128
NODES = 16
HEADS_DEV = 8
ROWS = HEADS_DEV * TOK
CHUNK = 256
F32 = jnp.float32
BF16 = jnp.bfloat16
INV_ROOT = 1.0 / math.sqrt(HD)


def z_moves(step):
    return [(2 * z + c, 2 * ((z + step * (1 - 2 * c)) % 8) + c) for z in range(8) for c in range(2)]


def y_moves(step):
    return [(8 * c + y, 8 * c + (y + step * (1 - 2 * c)) % 8) for c in range(2) for y in range(8)]


def dp_moves(first):
    return [
        (2 * x + c, 2 * ((x ^ 1) if (c == 0) == first else 3 - x) + c)
        for x in range(4)
        for c in range(2)
    ]


def along_z(x):
    return lax.ppermute(x, ("z", "core"), z_moves(1))


def back_z(x):
    return lax.ppermute(x, ("z", "core"), z_moves(-1))


def along_y(x):
    return lax.ppermute(x, ("core", "tensor"), y_moves(1))


def swap(x):
    return lax.ppermute(x, "core", [(0, 1), (1, 0)])


def dot(a, b, ca, cb):
    return lax.dot_general(a, b, (((ca,), (cb,)), ((), ())), preferred_element_type=F32)


def attend_kernel(par_ref, node_ref, q_ref, g_ref, kv_ref, att_ref, dq_ref, terms_ref,
                  s_scr, p_scr, qs, gs, q_t, g_t, mix_t, dq_t, blocks):
    node = node_ref[0]

    def follow(_, state):
        current, count = state

        @pl.when(current >= 0)
        def _():
            blocks[count] = current

        found = (current >= 0).astype(jnp.int32)
        parent = par_ref[0, jnp.maximum(current, 0)]
        return (jnp.where(current >= 0, parent, -1), count + found)

    blocks[0] = node
    _, count = lax.fori_loop(0, NODES - 1, follow, (par_ref[0, node], jnp.int32(1)))

    for h in range(HEADS_DEV):
        cols = slice(h * HD, (h + 1) * HD)
        rows = slice(h * TOK, (h + 1) * TOK)
        q_h = q_ref[:, cols]
        g_h = g_ref[:, cols]
        qs[rows, :] = q_h
        gs[rows, :] = g_h
        q_t[:, rows] = q_h.astype(F32).T.astype(BF16)
        g_t[:, rows] = g_h.astype(F32).T.astype(BF16)
    terms_ref[...] = jnp.zeros_like(terms_ref)
    mix_t[...] = jnp.zeros_like(mix_t)
    dq_t[...] = jnp.zeros_like(dq_t)

    chunks = [slice(c * CHUNK, (c + 1) * CHUNK) for c in range(ROWS // CHUNK)]
    key_pos = lax.broadcasted_iota(jnp.int32, (TOK, CHUNK), 0)
    query_pos = lax.broadcasted_iota(jnp.int32, (TOK, CHUNK), 1) % TOK
    causal = key_pos <= query_pos

    def fold(x, op):
        return op(x.reshape(TOK // 8, 8, CHUNK), axis=0)

    def rows_of(b):
        return pl.ds(pl.multiple_of(b * TOK, TOK), TOK)

    tops = []
    k_own = kv_ref[rows_of(node), :HD]
    for c in chunks:
        s = jnp.where(causal, dot(k_own, q_t[:, c], 1, 0) * INV_ROOT, -jnp.inf)
        s_scr[0, :, c] = s
        tops.append(fold(s, jnp.max))

    def score(i, tops):
        k_b = kv_ref[rows_of(blocks[i]), :HD]
        out = []
        for c, top in zip(chunks, tops):
            s = dot(k_b, q_t[:, c], 1, 0) * INV_ROOT
            s_scr[i, :, c] = s
            out.append(jnp.maximum(top, fold(s, jnp.max)))
        return tuple(out)

    tops = lax.fori_loop(1, count, score, tuple(tops))
    tops = [jnp.max(t, axis=0, keepdims=True) for t in tops]

    def expo(i, sums):
        out = []
        for c, top, total in zip(chunks, tops, sums):
            e = jnp.exp(s_scr[i, :, c] - top)
            s_scr[i, :, c] = e
            out.append(total + fold(e, jnp.sum))
        return tuple(out)

    sums = lax.fori_loop(0, count, expo, tuple(jnp.zeros((8, CHUNK), F32) for _ in chunks))
    invs = [1.0 / jnp.sum(t, axis=0, keepdims=True) for t in sums]

    def mix(i, _):
        v_b = kv_ref[rows_of(blocks[i]), HD:]
        for c, inv in zip(chunks, invs):
            p = s_scr[i, :, c] * inv
            s_scr[i, :, c] = p
            pb = p.astype(BF16)
            p_scr[i, :, c] = pb
            mix_t[:, c] += dot(v_b, pb, 0, 0)
        return 0

    lax.fori_loop(0, count, mix, 0)
    inners = [jnp.sum(g_t[:, c].astype(F32) * mix_t[:, c], axis=0, keepdims=True) for c in chunks]

    def back(i, _):
        b = rows_of(blocks[i])
        k_b = kv_ref[b, :HD]
        v_b = kv_ref[b, HD:]
        dk = jnp.zeros((TOK, HD), F32)
        dv = jnp.zeros((TOK, HD), F32)
        for c, inner in zip(chunks, inners):
            dp = dot(v_b, g_t[:, c], 1, 0)
            ds = (s_scr[i, :, c] * (dp - inner) * INV_ROOT).astype(BF16)
            dq_t[:, c] += dot(k_b, ds, 0, 0)
            dk += dot(ds, qs[c, :], 1, 0)
            dv += dot(p_scr[i, :, c], gs[c, :], 1, 0)
        terms_ref[b, :HD] = dk.astype(BF16)
        terms_ref[b, HD:] = dv.astype(BF16)
        return 0

    lax.fori_loop(0, count, back, 0)
    for h in range(HEADS_DEV):
        cols = slice(h * HD, (h + 1) * HD)
        rows = slice(h * TOK, (h + 1) * TOK)
        att_ref[:, cols] = mix_t[:, rows].T.astype(BF16)
        dq_ref[:, cols] = dq_t[:, rows].T


def attend(parents, node, queries, out_grad, kv):
    smem = pl.BlockSpec(memory_space=pltpu.SMEM)
    vmem = pl.BlockSpec(memory_space=pltpu.VMEM)
    group = NODES * TOK
    return pl.pallas_call(
        attend_kernel,
        out_shape=(
            jax.ShapeDtypeStruct((TOK, ROWS), BF16),
            jax.ShapeDtypeStruct((TOK, ROWS), F32),
            jax.ShapeDtypeStruct((group, 2 * HD), BF16),
        ),
        in_specs=[smem, smem, vmem, vmem, vmem],
        out_specs=(vmem, vmem, vmem),
        scratch_shapes=[
            pltpu.VMEM((NODES, TOK, ROWS), F32),
            pltpu.VMEM((NODES, TOK, ROWS), BF16),
            pltpu.VMEM((ROWS, HD), BF16),
            pltpu.VMEM((ROWS, HD), BF16),
            pltpu.VMEM((HD, ROWS), BF16),
            pltpu.VMEM((HD, ROWS), BF16),
            pltpu.VMEM((HD, ROWS), F32),
            pltpu.VMEM((HD, ROWS), F32),
            pltpu.SMEM((NODES,), jnp.int32),
        ],
        compiler_params=pltpu.CompilerParams(vmem_limit_bytes=40 << 20),
        name="attend",
    )(parents, node, queries, out_grad, kv)


def by_core(core, first, second):
    return jnp.where(core == 0, first, second)


def half_of(x, core, axis):
    size = x.shape[axis] // 2
    return lax.dynamic_slice_in_dim(x, core * size, size, axis)


def chip_pair(x, core):
    other = swap(x)
    return by_core(core, jnp.concatenate([x, other], 0), jnp.concatenate([other, x], 0))


def place_all(parts, places):
    whole = jnp.zeros((8,) + parts[0].shape, parts[0].dtype)
    for part, place in zip(parts, places):
        whole = lax.dynamic_update_slice_in_dim(whole, part[None], place % 8, 0)
    return whole


def relative(whole, own, core, side, axis):
    pick = lambda place: lax.dynamic_index_in_dim(whole, place % 8, 0, keepdims=False)
    parts = [half_of(pick(own), core, axis)]
    parts += [pick(own + side * r) for r in (1, 2, 3)]
    parts.append(half_of(pick(own + 4), core, axis))
    return parts


def ring_reduce(parts, core, subs):
    own, near, middle, far, last = parts
    size = last.shape[0]
    width = last.shape[1] // subs
    cols = [slice(i * width, (i + 1) * width) for i in range(subs)]
    moving = [back_z(last[:, c]) for c in cols]
    padded = []
    for m in moving:
        wide = jnp.zeros((2 * size, width), BF16)
        padded.append(lax.dynamic_update_slice_in_dim(wide, m, core * size, 0))
    moving = padded
    for part in (far, middle, near):
        moving = [back_z((part[:, c].astype(F32) + m.astype(F32)).astype(BF16)) for c, m in zip(cols, moving)]
    return jnp.concatenate(moving, axis=1)


def per_device(hidden, queries, kv_weight, parents, out_grad):
    core = lax.axis_index("core")
    z = lax.axis_index("z")
    y = lax.axis_index("tensor")
    side = 2 * core - 1
    node = (2 * z + core).astype(jnp.int32)[None]
    moved_h = chip_pair(hidden, core)
    moved_w = chip_pair(kv_weight, core)
    h_parts, h_places = [moved_h], [y]
    w_parts = [kv_weight]
    for r in (1, 2, 3):
        moved_h, moved_w = along_y(moved_h), along_z(moved_w)
        h_parts += [moved_h, swap(moved_h)]
        h_places += [y + side * r, y - side * r]
        w_parts.append(moved_w)
    last_h = along_y(half_of(moved_h, core, 1))
    w_parts.append(along_z(half_of(moved_w, core, 0)))
    other_h = swap(last_h)
    h_parts.append(by_core(core, jnp.concatenate([last_h, other_h], 1), jnp.concatenate([other_h, last_h], 1)))
    h_places.append(y + 4)
    h_mine = jnp.concatenate(relative(place_all(h_parts, h_places), z, core, side, 1), axis=1)
    partial = dot(h_mine, jnp.concatenate(w_parts, axis=0), 1, 0)
    kv = (partial + swap(partial)).astype(BF16)
    kv_parts, kv_places, moved = [kv], [z], kv
    for r in (1, 2, 3):
        moved = along_z(moved)
        kv_parts += [moved, swap(moved)]
        kv_places += [z + side * r, z - side * r]
    last = along_z(half_of(moved, core, 0))
    other = swap(last)
    kv_parts.append(by_core(core, jnp.concatenate([last, other], 0), jnp.concatenate([other, last], 0)))
    kv_places.append(z + 4)
    kv_all = place_all(kv_parts, kv_places).reshape(NODES * TOK, 2 * HD)
    attended, query_grad, terms = attend(parents, node, queries, out_grad, kv_all)
    terms = terms.reshape(8, 2 * TOK, 2 * HD)
    keep = jnp.concatenate(relative(terms, z, core, side, 0), axis=0)
    send = jnp.concatenate(relative(terms, z, 1 - core, -side, 0), axis=0)
    both = keep.astype(F32) + swap(send).astype(F32)
    both_parts = [both[a:b].astype(BF16) for a, b in ((0, 128), (128, 384), (384, 640), (640, 896), (896, 1024))]
    got = ring_reduce(both_parts, core, 1).astype(F32)
    own = lax.dynamic_update_slice_in_dim(jnp.zeros((2 * TOK, 2 * HD), F32), both[:TOK], core * TOK, 0)
    got = (got + own).astype(BF16)
    kv_grad = (got.astype(F32) + swap(got).astype(F32)).astype(BF16)
    local = dot(h_mine, kv_grad, 0, 0) * (1.0 / 64.0)
    local_parts = [local[a:b].astype(BF16) for a, b in ((0, 512), (512, 1536), (1536, 2560), (2560, 3584), (3584, 4096))]
    got = ring_reduce(local_parts, core, 2)
    other = swap(half_of(got, 1 - core, 0))
    total = (local[:512] + half_of(got, core, 0).astype(F32) + other.astype(F32)).astype(BF16)
    for first in (True, False):
        met = lax.ppermute(total, ("dp", "core"), dp_moves(first))
        summed = total.astype(F32) + met.astype(F32)
        total = summed.astype(BF16)
    return attended, query_grad, summed


def solution(mesh):
    fine = Mesh(mesh.devices.reshape(4, 8, 2, 8), ("dp", "z", "core", "tensor"))
    tokens = P(("dp", "z", "core"), "tensor")
    weight = P(("z", "core"), "tensor")
    return jax.shard_map(
        per_device,
        mesh=fine,
        in_specs=(tokens, tokens, weight, P("dp", None), tokens),
        out_specs=(tokens, tokens, weight),
        check_vma=False,
    )
```

```python
import math

import jax
import jax.numpy as jnp
from jax import lax
from jax.experimental import pallas as pl
from jax.experimental.pallas import tpu as pltpu
from jax.sharding import Mesh, PartitionSpec as P

HD = 128
TOK = 128
NODES = 16
HEADS_DEV = 8
ROWS = HEADS_DEV * TOK
CHUNK = 256
F32 = jnp.float32
BF16 = jnp.bfloat16
INV_ROOT = 1.0 / math.sqrt(HD)


def swap(x):
    return lax.ppermute(x, "core", [(0, 1), (1, 0)])


def dot(a, b, ca, cb):
    return lax.dot_general(a, b, (((ca,), (cb,)), ((), ())), preferred_element_type=F32)


def attend_kernel(par_ref, place_ref, q_ref, g_ref, mine_ref, other_ref, att_ref, dq_ref, keep_ref, send_ref,
                  s_scr, p_scr, qs, gs, q_t, g_t, mix_t, dq_t, blocks):
    node = place_ref[0]
    core = place_ref[1]

    def follow(_, state):
        current, count = state

        @pl.when(current >= 0)
        def _():
            blocks[count] = current

        found = (current >= 0).astype(jnp.int32)
        parent = par_ref[0, jnp.maximum(current, 0)]
        return (jnp.where(current >= 0, parent, -1), count + found)

    blocks[0] = node
    _, count = lax.fori_loop(0, NODES - 1, follow, (par_ref[0, node], jnp.int32(1)))

    for h in range(HEADS_DEV):
        cols = slice(h * HD, (h + 1) * HD)
        rows = slice(h * TOK, (h + 1) * TOK)
        q_h = q_ref[:, cols]
        g_h = g_ref[:, cols]
        qs[rows, :] = q_h
        gs[rows, :] = g_h
        q_t[:, rows] = q_h.astype(F32).T.astype(BF16)
        g_t[:, rows] = g_h.astype(F32).T.astype(BF16)
    keep_ref[...] = jnp.zeros_like(keep_ref)
    send_ref[...] = jnp.zeros_like(send_ref)
    mix_t[...] = jnp.zeros_like(mix_t)
    dq_t[...] = jnp.zeros_like(dq_t)

    chunks = [slice(c * CHUNK, (c + 1) * CHUNK) for c in range(ROWS // CHUNK)]
    key_pos = lax.broadcasted_iota(jnp.int32, (TOK, CHUNK), 0)
    query_pos = lax.broadcasted_iota(jnp.int32, (TOK, CHUNK), 1) % TOK
    causal = key_pos <= query_pos

    def fold(x, op):
        return op(x.reshape(TOK // 8, 8, CHUNK), axis=0)

    def pair(b, cols):
        z = b // 2
        return jnp.where(b % 2 == core, mine_ref[z, :, cols], other_ref[z, :, cols])

    key_cols, value_cols = slice(0, HD), slice(HD, 2 * HD)

    tops = []
    k_own = pair(node, key_cols)
    for c in chunks:
        s = jnp.where(causal, dot(k_own, q_t[:, c], 1, 0) * INV_ROOT, -jnp.inf)
        s_scr[0, :, c] = s
        tops.append(fold(s, jnp.max))

    def score(i, tops):
        k_b = pair(blocks[i], key_cols)
        out = []
        for c, top in zip(chunks, tops):
            s = dot(k_b, q_t[:, c], 1, 0) * INV_ROOT
            s_scr[i, :, c] = s
            out.append(jnp.maximum(top, fold(s, jnp.max)))
        return tuple(out)

    tops = lax.fori_loop(1, count, score, tuple(tops))
    tops = [jnp.max(t, axis=0, keepdims=True) for t in tops]

    def expo(i, sums):
        out = []
        for c, top, total in zip(chunks, tops, sums):
            e = jnp.exp(s_scr[i, :, c] - top)
            s_scr[i, :, c] = e
            out.append(total + fold(e, jnp.sum))
        return tuple(out)

    sums = lax.fori_loop(0, count, expo, tuple(jnp.zeros((8, CHUNK), F32) for _ in chunks))
    invs = [1.0 / jnp.sum(t, axis=0, keepdims=True) for t in sums]

    def mix(i, _):
        v_b = pair(blocks[i], value_cols)
        for c, inv in zip(chunks, invs):
            p = s_scr[i, :, c] * inv
            s_scr[i, :, c] = p
            pb = p.astype(BF16)
            p_scr[i, :, c] = pb
            mix_t[:, c] += dot(v_b, pb, 0, 0)
        return 0

    lax.fori_loop(0, count, mix, 0)
    inners = [jnp.sum(g_t[:, c].astype(F32) * mix_t[:, c], axis=0, keepdims=True) for c in chunks]

    def back(i, _):
        b = blocks[i]
        k_b = pair(b, key_cols)
        v_b = pair(b, value_cols)
        dk = jnp.zeros((TOK, HD), F32)
        dv = jnp.zeros((TOK, HD), F32)
        for c, inner in zip(chunks, inners):
            dp = dot(v_b, g_t[:, c], 1, 0)
            ds = (s_scr[i, :, c] * (dp - inner) * INV_ROOT).astype(BF16)
            dq_t[:, c] += dot(k_b, ds, 0, 0)
            dk += dot(ds, qs[c, :], 1, 0)
            dv += dot(p_scr[i, :, c], gs[c, :], 1, 0)

        def store(ref):
            ref[b // 2, :, :HD] = dk.astype(BF16)
            ref[b // 2, :, HD:] = dv.astype(BF16)

        pl.when(b % 2 == core)(lambda: store(keep_ref))
        pl.when(b % 2 != core)(lambda: store(send_ref))
        return 0

    lax.fori_loop(0, count, back, 0)
    for h in range(HEADS_DEV):
        cols = slice(h * HD, (h + 1) * HD)
        rows = slice(h * TOK, (h + 1) * TOK)
        att_ref[:, cols] = mix_t[:, rows].T.astype(BF16)
        dq_ref[:, cols] = dq_t[:, rows].T


def attend(parents, place, queries, out_grad, mine, other):
    smem = pl.BlockSpec(memory_space=pltpu.SMEM)
    vmem = pl.BlockSpec(memory_space=pltpu.VMEM)
    half = jax.ShapeDtypeStruct((NODES // 2, TOK, 2 * HD), BF16)
    return pl.pallas_call(
        attend_kernel,
        out_shape=(
            jax.ShapeDtypeStruct((TOK, ROWS), BF16),
            jax.ShapeDtypeStruct((TOK, ROWS), F32),
            half,
            half,
        ),
        in_specs=[smem, smem, vmem, vmem, vmem, vmem],
        out_specs=(vmem, vmem, vmem, vmem),
        scratch_shapes=[
            pltpu.VMEM((NODES, TOK, ROWS), F32),
            pltpu.VMEM((NODES, TOK, ROWS), BF16),
            pltpu.VMEM((ROWS, HD), BF16),
            pltpu.VMEM((ROWS, HD), BF16),
            pltpu.VMEM((HD, ROWS), BF16),
            pltpu.VMEM((HD, ROWS), BF16),
            pltpu.VMEM((HD, ROWS), F32),
            pltpu.VMEM((HD, ROWS), F32),
            pltpu.SMEM((NODES,), jnp.int32),
        ],
        compiler_params=pltpu.CompilerParams(vmem_limit_bytes=40 << 20),
        name="attend",
    )(parents, place, queries, out_grad, mine, other)


def in_order(core, mine, other, axis):
    return jnp.where(
        core == 0, jnp.concatenate([mine, other], axis), jnp.concatenate([other, mine], axis)
    )


def share(x, axis, size):
    return lax.all_to_all(jnp.broadcast_to(x[None], (size,) + x.shape), axis, 0, 0, tiled=True)


def per_device(hidden, queries, kv_weight, parents, out_grad):
    core = lax.axis_index("core")
    place = jnp.stack([lax.axis_index("z") * 2 + core, core]).astype(jnp.int32)
    weight_all = share(kv_weight, "z", 8)
    width = hidden.shape[1] // 2
    mine = lax.dynamic_slice_in_dim(hidden, core * width, width, 1)
    sent = lax.dynamic_slice_in_dim(hidden, (1 - core) * width, width, 1)
    hidden_all = share(in_order(core, mine, swap(sent), 0), "tensor", 8)
    partial = lax.dot_general(
        hidden_all, weight_all, (((0, 2), (0, 1)), ((), ())), preferred_element_type=F32
    )
    kv = (partial + swap(partial)).astype(BF16)
    kv_mine = share(lax.dynamic_slice_in_dim(kv, core * TOK, TOK, 0), "z", 8)
    attended, query_grad, keep, send = attend(
        parents, place, queries, out_grad, kv_mine, swap(kv_mine)
    )
    terms = (keep.astype(F32) + swap(send).astype(F32)).astype(BF16)
    terms = lax.all_to_all(terms, "z", 0, 0, tiled=True)
    kv_grad = jnp.sum(terms.astype(F32), axis=0).astype(BF16)
    kv_grad = in_order(core, kv_grad, swap(kv_grad), 0)
    local = lax.dot_general(
        hidden_all, kv_grad, (((1,), (0,)), ((), ())), preferred_element_type=F32
    )
    local = (local * (1.0 / 64.0)).astype(BF16).reshape(8, 4, 128, 256).transpose(1, 0, 2, 3)
    sums = lax.all_to_all(local.reshape(32, 128, 256), ("dp", "z"), 0, 0, tiled=True)
    quarter = jnp.sum(sums.astype(F32), axis=0).astype(BF16)
    return attended, query_grad, share(quarter, "dp", 4).reshape(512, 256).astype(F32)


def solution(mesh):
    fine = Mesh(mesh.devices.reshape(4, 8, 2, 8), ("dp", "z", "core", "tensor"))
    tokens = P(("dp", "z", "core"), "tensor")
    weight = P(("z", "core"), "tensor")
    return jax.shard_map(
        per_device,
        mesh=fine,
        in_specs=(tokens, tokens, weight, P("dp", None), tokens),
        out_specs=(tokens, tokens, weight),
        check_vma=False,
    )
```
